32 devices in a mesh: dp: 8 (over z, y), tensor: 4 (over x, core).
Axes of the slice: x: 2, y: 2, z: 4, core: 2. Of those that a mesh axis runs over, the one named last changes fastest.
Arguments:
- tokens: bfloat16 [2, 128, 12288], P(None, 'dp', 'tensor'), may hold values from -6 to 6
- up_weight: bfloat16 [12288, 49152], P('tensor', 'dp'), may hold values from -0.0546875 to 0.0546875
- up_bias: bfloat16 [49152], P('dp'), may hold values from -3 to 3
- down_weight: bfloat16 [49152, 12288], P('dp', 'tensor'), may hold values from -0.02734375 to 0.02734375
- down_bias: bfloat16 [12288], P('tensor'), may hold values from -3 to 3
- active: int32 [2, 1, 384], P(None, None, 'dp'), may hold values from 0 to 1
Outputs:
- mixed: bfloat16 [2, 128, 12288], P(None, 'dp', 'tensor')
The draws below stay inside these ranges and needn't reach their ends.
All inputs are finite; a program needn't handle non-finite values.
Results may differ from the reference program's by a relative error of at most 0.0042.
Values may be sent and summed in bfloat16 or wider, within the bound.
A program may use at most 128 MiB of HBM per device.

```python
import jax
import jax.numpy as jnp

D = 12288
FF = 49152
HBLK = 128
RBLK = 128
STEPS = 2
ROWS = 128


def draw_active(key, part):
    groups = FF // HBLK // 4
    levels = jax.random.randint(jax.random.fold_in(key, 11), (groups,), 1, 8)
    coins = jax.random.randint(jax.random.fold_in(key, 12), (STEPS, ROWS // RBLK, FF // HBLK), 0, 8)
    return (coins < jnp.repeat(levels, 4)[None, None, :]).astype(jnp.int32)


def shard_levels(rng, extent, pieces, low, high):
    loudness = 1.0
    for position, parts in pieces:
        heights = jax.random.uniform(jax.random.fold_in(jax.random.fold_in(rng, 6), position), (parts,), jnp.float32, low / len(pieces), high / len(pieces))
        loudness = loudness * jnp.repeat(jnp.exp(heights), extent[position] // parts).reshape((-1,) + (1,) * (len(extent) - 1 - position))
    return loudness


def gaussian(key, dims, spread, reach, cuts=(), held_as=jnp.bfloat16):
    result = jax.random.normal(key, dims, jnp.float32) * spread
    if len(cuts) > 0:
        result = shard_levels(key, dims, cuts, -0.22, 0.18) * result
    return jnp.clip(result, min=-reach, max=reach).astype(held_as)


def setup_inputs(seed: int = 0) -> dict:
    splits = jax.random.split(jax.random.key(seed), 7)
    tokens = gaussian(splits[0], (STEPS, ROWS, D), 1.0, 6.0, ((1, 8), (2, 4)))
    up_weight = gaussian(splits[1], (D, FF), D ** -0.5, 0.0546875, ((0, 4), (1, 8)))
    up_bias = gaussian(splits[2], (FF,), 0.5, 3.0, ((0, 8),))
    down_weight = gaussian(splits[3], (FF, D), FF ** -0.5, 0.02734375, ((0, 8), (1, 4)))
    down_bias = gaussian(splits[4], (D,), 0.5, 3.0, ((0, 4),))
    active = draw_active(jax.random.fold_in(splits[6], 71), 0)
    return {"tokens": tokens, "up_weight": up_weight, "up_bias": up_bias, "down_weight": down_weight, "down_bias": down_bias, "active": active}


def reference(tokens, up_weight, up_bias, down_weight, down_bias, active):
    results = []
    for step_index in range(STEPS):
        preact = jnp.dot(tokens[step_index], up_weight, preferred_element_type=jnp.float32) + up_bias.astype(jnp.float32)
        row_mask = jnp.repeat(jnp.repeat(active[step_index].astype(jnp.float32), RBLK, axis=0), HBLK, axis=1)
        hidden = (jnp.maximum(preact, 0.0) * row_mask).astype(jnp.bfloat16)
        summed = jnp.dot(hidden, down_weight, preferred_element_type=jnp.float32) + down_bias.astype(jnp.float32)
        results.append(summed.astype(jnp.bfloat16))
    return jnp.stack(results)
```

```python
import functools

import jax
import jax.numpy as jnp
from jax import lax
from jax.experimental import pallas as pl
from jax.experimental.pallas import tpu as pltpu
from jax.sharding import PartitionSpec as P

RBLK = 128
TILE = 512
MESH = pl.DeviceIdType.MESH


def activate(summed, up_bias, mask_table, first_row):
    row_count = summed.shape[0]
    blocks = mask_table.shape[1]
    row_ids = first_row + jnp.arange(row_count, dtype=jnp.int32)
    onehot = (
        row_ids[:, None] // RBLK == jnp.arange(mask_table.shape[0], dtype=jnp.int32)[None, :]
    ).astype(jnp.float32)
    row_mask = jnp.dot(onehot, mask_table.astype(jnp.float32))
    preact = jnp.maximum(summed + up_bias.astype(jnp.float32), 0.0)
    gated_rows = preact.reshape(row_count, blocks, -1) * row_mask[:, :, None]
    return gated_rows.reshape(row_count, -1).astype(jnp.bfloat16)


def local(tokens, up_weight, up_bias, down_weight, down_bias, active):
    results = []
    for step_index in range(tokens.shape[0]):
        local_rows = tokens[step_index]
        mask_table = active[step_index]
        partial_up = jnp.dot(
            lax.all_gather(local_rows, "dp", axis=0, tiled=True),
            up_weight,
            preferred_element_type=jnp.float32,
        )
        row_share = lax.psum_scatter(partial_up, "tensor", scatter_dimension=0, tiled=True)
        first_row = lax.axis_index("tensor") * row_share.shape[0]
        hidden_share = activate(row_share, up_bias, mask_table, first_row)
        hidden = lax.all_gather(hidden_share, "tensor", axis=0, tiled=True)
        mixed_rows = lax.psum_scatter(
            jnp.dot(hidden, down_weight, preferred_element_type=jnp.float32),
            "dp",
            scatter_dimension=0,
            tiled=True,
        )
        results.append((mixed_rows + down_bias.astype(jnp.float32)).astype(jnp.bfloat16))
    return jnp.stack(results)


def fused_kernel(nz, nt, tok, wu, wd, bias_u, mask, bias_d, out,
                 x_all, w, pbuf, crecv, xsend, xrecv, hid, acc, ysend, yrecv, zsend, zrecv,
                 tsem, wsem, ag_send, ag_recv, c_send, c_recv, x_send, x_recv, h_send, h_recv,
                 y_send, y_recv, z_send, z_recv):
    f32, bf16 = jnp.float32, jnp.bfloat16
    steps, share, depth = tok.shape
    rows = x_all.shape[1]
    half = rows // 2
    dp, t = lax.axis_index("dp"), lax.axis_index("tensor")
    z, y = dp // 2, dp % 2
    x, c = t // 2, t % 2
    y_peer = (z * 2 + 1 - y, t)
    x_peer = (dp, (1 - x) * 2 + c)
    c_peer = (dp, x * 2 + 1 - c)
    z_of = lambda k: lax.rem(z + k, nz)
    own = pl.ds(pl.multiple_of(c * half, half), half)
    other = pl.ds(pl.multiple_of((1 - c) * half, half), half)
    block = lambda d: pl.ds(pl.multiple_of(d * share, share), share)

    def rcopy(src, dst, ss, rs, dev):
        return pltpu.make_async_remote_copy(
            src_ref=src, dst_ref=dst, send_sem=ss, recv_sem=rs, device_id=dev, device_id_type=MESH
        )

    def up_load(j):
        cols = pl.ds(pl.multiple_of(j * TILE, TILE), TILE)
        return pltpu.make_async_copy(wu.at[:, cols], w.at[j], wsem.at[j])

    def down_load(j):
        lines = pl.ds(pl.multiple_of(j * TILE, TILE), TILE)
        for n in range(depth // TILE):
            part = pl.ds(n * TILE, TILE)
            pltpu.make_async_copy(wd.at[lines, part], w.at[j, part], wsem.at[j]).start()

    mine = [pltpu.make_async_copy(tok.at[s], x_all.at[s, block(dp)], tsem.at[s]) for s in range(steps)]
    for copy in mine:
        copy.start()

    @pl.loop(0, nt)
    def _(j):
        up_load(j).start()

    barrier = pltpu.get_barrier_semaphore()
    peers = [y_peer, x_peer, c_peer] + [(z_of(k) * 2 + y, t) for k in range(1, nz)]
    for peer in peers:
        pl.semaphore_signal(barrier, inc=1, device_id=peer, device_id_type=MESH)
    pl.semaphore_wait(barrier, len(peers))

    def ag_copy(s, k, d, peer):
        view = x_all.at[s, block(d)]
        return rcopy(view, view, ag_send.at[s, k], ag_recv.at[s, d], peer)

    def ag_sends(s):
        mine[s].wait()
        ag_copy(s, 0, dp, y_peer).start()
        for k in range(1, nz):
            ag_copy(s, k, dp, (z_of(k) * 2 + y, t)).start()

    def ag_forward(s):
        for k in range(1, nz):
            d = z_of(k) * 2 + y
            ag_copy(s, k, d, y_peer).wait_recv()
            ag_copy(s, nz - 1 + k, d, y_peer).start()

    def ag_finish(s):
        for k in range(nz):
            ag_copy(s, k, z_of(k) * 2 + 1 - y, y_peer).wait_recv()

    def c_copy(q):
        return rcopy(pbuf.at[q, other], crecv.at[q], c_send.at[q], c_recv.at[q], c_peer)

    def x_copy(q):
        return rcopy(xsend.at[q], xrecv.at[q], x_send.at[q], x_recv.at[q], x_peer)

    def h_copy(q, lines):
        return rcopy(hid.at[q, lines], hid.at[q, lines], h_send.at[q], h_recv.at[q], c_peer)

    def up(s, j):
        q = s * nt + j
        pbuf[q] = jnp.dot(x_all[s], w[j], preferred_element_type=f32)
        c_copy(q).start()

    def mid(q):
        c_copy(q).wait_recv()
        total = pbuf[q, own] + crecv[q]
        crecv[q] = total
        xsend[q] = total.astype(bf16)
        x_copy(q).start()

    def act(s, j):
        q = s * nt + j
        x_copy(q).wait_recv()
        pre = crecv[q] + xrecv[q].astype(f32) + bias_u[j]
        hid[q, own] = (jnp.maximum(pre, 0.0) * mask[q]).astype(bf16)
        h_copy(q, own).start()

    def down(s, j):
        q = s * nt + j
        h_copy(q, other).wait_recv()
        rows_in = hid[q]
        for n in range(depth // TILE):
            part = pl.ds(n * TILE, TILE)
            acc[s, :, part] += jnp.dot(rows_in, w[j, part], preferred_element_type=f32)

    def y_copy(s, k):
        i = s * nz + k
        return rcopy(ysend.at[i], yrecv.at[i], y_send.at[i], y_recv.at[i], y_peer)

    def z_copy(s, k):
        i = s * nz + k
        return rcopy(zsend.at[i], zrecv.at[i], z_send.at[i], z_recv.at[i], (z_of(k) * 2 + y, t))

    def rs_y(s):
        for k in [*range(1, nz), 0]:
            ysend[s * nz + k] = acc[s, block(z_of(k) * 2 + 1 - y)].astype(bf16)
            y_copy(s, k).start()

    def rs_z(s):
        for k in range(1, nz):
            y_copy(s, k).wait_recv()
            pair = acc[s, block(z_of(k) * 2 + y)] + yrecv[s * nz + k].astype(f32)
            zsend[s * nz + k] = pair.astype(bf16)
            z_copy(s, k).start()

    def rs_finish(s):
        y_copy(s, 0).wait_recv()
        total = acc[s, block(dp)] + yrecv[s * nz].astype(f32)
        for k in range(1, nz):
            z_copy(s, k).wait_recv()
            total += zrecv[s * nz + k].astype(f32)
        out[s] = (total + bias_d[...]).astype(bf16)

    ag_sends(0)
    ag_forward(0)
    ag_sends(1)
    acc[...] = jnp.zeros_like(acc)
    ag_finish(0)
    part_way = nt * 2 // 3

    def first_step(j):
        up_load(j).wait()
        up(0, j)

        @pl.when(j >= 1)
        def _():
            mid(j - 1)

    pl.loop(0, part_way)(first_step)
    ag_forward(1)
    pl.loop(part_way, nt)(first_step)
    mid(nt - 1)
    ag_finish(1)

    @pl.loop(0, nt)
    def _(j):
        up(1, j)

        @pl.when(j >= 1)
        def _():
            mid(nt + j - 1)
            down_load(j - 1)

        act(0, j)

    mid(2 * nt - 1)
    down_load(nt - 1)

    @pl.loop(0, nt)
    def _(j):
        up_load(j).wait()
        down(0, j)

    rs_y(0)
    ahead = nt // 3

    @pl.loop(0, ahead)
    def _(j):
        act(1, j)

    rs_z(0)

    @pl.loop(0, ahead - 1)
    def _(j):
        down(1, j)

    @pl.loop(ahead, nt)
    def _(j):
        act(1, j)
        down(1, j - 1)

    down(1, nt - 1)
    rs_y(1)
    rs_finish(0)
    rs_z(1)
    rs_finish(1)

    for s in range(steps):
        for k in range(2 * nz - 1):
            ag_copy(s, k, dp, y_peer).wait_send()
        for k in range(nz):
            y_copy(s, k).wait_send()
        for k in range(1, nz):
            z_copy(s, k).wait_send()

    @pl.loop(0, steps * nt)
    def _(q):
        c_copy(q).wait_send()
        x_copy(q).wait_send()
        h_copy(q, own).wait_send()


def fused(groups, tokens, up_weight, up_bias, down_weight, down_bias, active):
    steps, share, depth = tokens.shape
    hidden = up_weight.shape[1]
    rows, nz, nt = groups * share, groups // 2, hidden // TILE
    f32, bf16 = jnp.float32, jnp.bfloat16
    width = hidden // active.shape[2]
    mask = jnp.repeat(active.astype(f32).reshape(steps, -1), width, axis=1).reshape(steps * nt, 1, TILE)
    any_space, vmem = pl.BlockSpec(memory_space=pl.ANY), pl.BlockSpec(memory_space=pltpu.VMEM)
    dma = pltpu.SemaphoreType.DMA
    half = rows // 2
    return pl.pallas_call(
        functools.partial(fused_kernel, nz, nt),
        out_shape=jax.ShapeDtypeStruct(tokens.shape, bf16),
        in_specs=[any_space, any_space, any_space, vmem, vmem, vmem],
        out_specs=vmem,
        scratch_shapes=[
            pltpu.VMEM((steps, rows, depth), bf16),
            pltpu.VMEM((nt, depth, TILE), bf16),
            pltpu.VMEM((steps * nt, rows, TILE), f32),
            pltpu.VMEM((steps * nt, half, TILE), f32),
            pltpu.VMEM((steps * nt, half, TILE), bf16),
            pltpu.VMEM((steps * nt, half, TILE), bf16),
            pltpu.VMEM((steps * nt, rows, TILE), bf16),
            pltpu.VMEM((steps, rows, depth), f32),
        ]
        + [pltpu.VMEM((steps * nz, share, depth), bf16)] * 4
        + [
            dma((steps,)),
            dma((nt,)),
            dma((steps, 2 * nz - 1)),
            dma((steps, 2 * nz)),
        ]
        + [dma((steps * nt,))] * 6
        + [dma((steps * nz,))] * 4,
        compiler_params=pltpu.CompilerParams(
            collective_id=0, has_side_effects=True, vmem_limit_bytes=67043328
        ),
    )(
        tokens,
        up_weight,
        down_weight,
        up_bias.astype(f32).reshape(nt, 1, TILE),
        mask,
        down_bias.astype(f32).reshape(1, depth),
    )


def solution(mesh):
    placed = (
        P(None, "dp", "tensor"),
        P("tensor", "dp"),
        P("dp"),
        P("dp", "tensor"),
        P("tensor"),
        P(None, None, "dp"),
    )
    groups, columns = mesh.shape["dp"], mesh.shape["tensor"]

    def body(*args):
        steps, share, depth = args[0].shape
        hidden, table = args[1].shape[1], args[5].shape
        if (
            (groups, columns, steps, table[1]) == (8, 4, 2, 1)
            and share % 16 == 0
            and depth % TILE == 0
            and hidden % TILE == 0
        ):
            return fused(groups, *args)
        return local(*args)

    return jax.shard_map(
        body, mesh=mesh, in_specs=placed, out_specs=P(None, "dp", "tensor"), check_vma=False
    )
```

```python
import functools

import jax
import jax.numpy as jnp
from jax import lax
from jax.experimental import pallas as pl
from jax.experimental.pallas import tpu as pltpu
from jax.sharding import PartitionSpec as P

RBLK = 128
TILE = 512
LAG = 3
MESH = pl.DeviceIdType.MESH


def activate(summed, up_bias, mask_table, first_row):
    row_count = summed.shape[0]
    blocks = mask_table.shape[1]
    row_ids = first_row + jnp.arange(row_count, dtype=jnp.int32)
    onehot = (
        row_ids[:, None] // RBLK == jnp.arange(mask_table.shape[0], dtype=jnp.int32)[None, :]
    ).astype(jnp.float32)
    row_mask = jnp.dot(onehot, mask_table.astype(jnp.float32))
    preact = jnp.maximum(summed + up_bias.astype(jnp.float32), 0.0)
    gated_rows = preact.reshape(row_count, blocks, -1) * row_mask[:, :, None]
    return gated_rows.reshape(row_count, -1).astype(jnp.bfloat16)


def local(tokens, up_weight, up_bias, down_weight, down_bias, active):
    results = []
    for step_index in range(tokens.shape[0]):
        local_rows = tokens[step_index]
        mask_table = active[step_index]
        partial_up = jnp.dot(
            lax.all_gather(local_rows, "dp", axis=0, tiled=True),
            up_weight,
            preferred_element_type=jnp.float32,
        )
        row_share = lax.psum_scatter(partial_up, "tensor", scatter_dimension=0, tiled=True)
        first_row = lax.axis_index("tensor") * row_share.shape[0]
        hidden_share = activate(row_share, up_bias, mask_table, first_row)
        hidden = lax.all_gather(hidden_share, "tensor", axis=0, tiled=True)
        mixed_rows = lax.psum_scatter(
            jnp.dot(hidden, down_weight, preferred_element_type=jnp.float32),
            "dp",
            scatter_dimension=0,
            tiled=True,
        )
        results.append((mixed_rows + down_bias.astype(jnp.float32)).astype(jnp.bfloat16))
    return jnp.stack(results)


def fused_kernel(nz, nt, tok, wu, wd, bias_u, active, out,
                 x_all, w, pbuf, crecv, xsend, xrecv, hid, acc, ysend, yrecv, zsend, zrecv,
                 tsem, wsem, ag_send, ag_recv, c_send, c_recv, x_send, x_recv, h_send, h_recv,
                 y_send, y_recv, z_send, z_recv):
    f32, bf16 = jnp.float32, jnp.bfloat16
    steps, share, depth = tok.shape
    rows = x_all.shape[1]
    half = rows // 2
    dp, t = lax.axis_index("dp"), lax.axis_index("tensor")
    z, y = dp // 2, dp % 2
    x, c = t // 2, t % 2
    y_peer = (z * 2 + 1 - y, t)
    x_peer = (dp, (1 - x) * 2 + c)
    c_peer = (dp, x * 2 + 1 - c)
    z_of = lambda k: lax.rem(z + k, nz)
    own = pl.ds(pl.multiple_of(c * half, half), half)
    other = pl.ds(pl.multiple_of((1 - c) * half, half), half)
    cols = lambda j: pl.ds(pl.multiple_of(j * TILE, TILE), TILE)
    nc = depth // TILE
    spans = nt // nc
    block = lambda d: pl.ds(pl.multiple_of(d * share, share), share)

    def rcopy(src, dst, ss, rs, dev):
        return pltpu.make_async_remote_copy(
            src_ref=src, dst_ref=dst, send_sem=ss, recv_sem=rs, device_id=dev, device_id_type=MESH
        )

    def up_load(j):
        return pltpu.make_async_copy(wu.at[:, cols(j)], w.at[j], wsem.at[j])

    def down_load(i):
        n, part = i // spans, i % spans
        lines = pl.ds(pl.multiple_of(part * depth, depth), depth)
        return pltpu.make_async_copy(wd.at[lines, cols(n)], w.at[i], wsem.at[i])

    mine = [pltpu.make_async_copy(tok.at[s], x_all.at[s, block(dp)], tsem.at[s]) for s in range(steps)]
    for copy in mine:
        copy.start()

    @pl.loop(0, nt)
    def _(j):
        up_load(j).start()

    barrier = pltpu.get_barrier_semaphore()
    peers = [y_peer, x_peer, c_peer] + [(z_of(k) * 2 + y, t) for k in range(1, nz)]
    for peer in peers:
        pl.semaphore_signal(barrier, inc=1, device_id=peer, device_id_type=MESH)
    pl.semaphore_wait(barrier, len(peers))

    def ag_copy(s, k, d, peer):
        view = x_all.at[s, block(d)]
        return rcopy(view, view, ag_send.at[s, k], ag_recv.at[s, d], peer)

    def ag_sends(s):
        mine[s].wait()
        ag_copy(s, 0, dp, y_peer).start()
        for k in range(1, nz):
            ag_copy(s, k, dp, (z_of(k) * 2 + y, t)).start()

    def ag_forward(s, k):
        d = z_of(k) * 2 + y
        ag_copy(s, k, d, y_peer).wait_recv()
        ag_copy(s, nz - 1 + k, d, y_peer).start()

    def ag_finish(s):
        for k in range(nz):
            ag_copy(s, k, z_of(k) * 2 + 1 - y, y_peer).wait_recv()

    def c_copy(q):
        return rcopy(pbuf.at[q, other], crecv.at[q], c_send.at[q], c_recv.at[q], c_peer)

    def x_copy(q):
        return rcopy(xsend.at[q], xrecv.at[q], x_send.at[q], x_recv.at[q], x_peer)

    def h_copy(s, j, lines):
        view, q = hid.at[s, lines, cols(j)], s * nt + j
        return rcopy(view, view, h_send.at[q], h_recv.at[q], c_peer)

    def up(s, j):
        q = s * nt + j
        pbuf[q] = jnp.dot(x_all[s], w[j], preferred_element_type=f32)
        c_copy(q).start()

    def mid(q):
        c_copy(q).wait_recv()
        total = pbuf[q, own] + crecv[q]
        crecv[q] = total
        xsend[q] = total.astype(bf16)
        x_copy(q).start()

    def act(s, j):
        q = s * nt + j
        x_copy(q).wait_recv()
        bias = bias_u[cols(j)].astype(f32).reshape(1, TILE)
        pre = jnp.maximum(crecv[q] + xrecv[q].astype(f32) + bias, 0.0)
        blocks = active.shape[2] // nt
        width = TILE // blocks
        for b in range(blocks):
            gate = active[s, 0, j * blocks + b].astype(f32)
            lanes = pl.ds(pl.multiple_of(j * TILE + b * width, width), width)
            hid[s, own, lanes] = (pre[:, b * width : (b + 1) * width] * gate).astype(bf16)
        h_copy(s, j, own).start()

    def hidden_ready(s):
        @pl.loop(0, nt)
        def _(j):
            h_copy(s, j, other).wait_recv()

    def y_copy(i):
        return rcopy(ysend.at[i], yrecv.at[i], y_send.at[i], y_recv.at[i], y_peer)

    def z_copy(i, k):
        q = i * nz + k
        return rcopy(zsend.at[q], zrecv.at[q], z_send.at[q], z_recv.at[q], (z_of(k) * 2 + y, t))

    def down(s, n):
        total = jnp.zeros((rows, TILE), f32)
        for part in range(spans):
            total += jnp.dot(
                hid[s, :, part * depth : (part + 1) * depth], w[n * spans + part], preferred_element_type=f32
            )
        acc[s, :, cols(n)] = total
        i = s * nc + n
        for zz in range(nz):
            ysend[i, zz] = acc[s, block(zz * 2 + 1 - y), cols(n)].astype(bf16)
        y_copy(i).start()

    def rs_z(s, n):
        i = s * nc + n
        y_copy(i).wait_recv()
        for k in range(1, nz):
            pair = acc[s, block(z_of(k) * 2 + y), cols(n)] + yrecv[i, z_of(k)].astype(f32)
            zsend[i * nz + k] = pair.astype(bf16)
            z_copy(i, k).start()

    def rs_finish(s, n):
        i = s * nc + n
        total = acc[s, block(dp), cols(n)] + yrecv[i, z].astype(f32)
        for k in range(1, nz):
            z_copy(i, k).wait_recv()
            total += zrecv[i * nz + k].astype(f32)
        out[s, :, cols(n)] = total

    ag_sends(0)
    for k in range(1, nz):
        ag_forward(0, k)
    ag_sends(1)
    ag_finish(0)

    def first_step(j):
        up_load(j).wait()
        up(0, j)

        @pl.when(j >= 1)
        def _():
            mid(j - 1)

    cut = [nt * k // (nz + 1) for k in range(nz)] + [nt]
    for k in range(nz):
        pl.loop(cut[k], cut[k + 1])(first_step)
        if k + 1 < nz:
            ag_forward(1, k + 1)
    mid(nt - 1)
    ag_finish(1)

    @pl.loop(0, nt)
    def _(j):
        up(1, j)

        @pl.when(j >= 1)
        def _():
            mid(nt + j - 1)
            down_load(j - 1).start()

        act(0, j)

    mid(2 * nt - 1)
    down_load(nt - 1).start()
    hidden_ready(0)

    @pl.loop(0, nc)
    def _(n):
        for part in range(spans):
            down_load(n * spans + part).wait()
        down(0, n)

        @pl.when(n >= LAG)
        def _():
            rs_z(0, n - LAG)

    @pl.loop(0, nt // 2)
    def _(j):
        act(1, j)

    @pl.loop(nc - LAG, nc)
    def _(n):
        rs_z(0, n)

    @pl.loop(nt // 2, nt)
    def _(j):
        act(1, j)

    hidden_ready(1)

    @pl.loop(0, nc)
    def _(n):
        down(1, n)

        @pl.when(n >= LAG)
        def _():
            rs_z(1, n - LAG)

    @pl.loop(nc - LAG, nc)
    def _(n):
        rs_z(1, n)

    for s in range(steps):
        @pl.loop(0, nc)
        def _(n):
            rs_finish(s, n)

    for s in range(steps):
        for k in range(2 * nz - 1):
            ag_copy(s, k, dp, y_peer).wait_send()

    @pl.loop(0, steps * nc)
    def _(i):
        y_copy(i).wait_send()
        for k in range(1, nz):
            z_copy(i, k).wait_send()

    for s in range(steps):
        @pl.loop(0, nt)
        def _(j):
            c_copy(s * nt + j).wait_send()
            x_copy(s * nt + j).wait_send()
            h_copy(s, j, own).wait_send()


def fused(groups, tokens, up_weight, up_bias, down_weight, down_bias, active):
    steps, share, depth = tokens.shape
    hidden = up_weight.shape[1]
    rows, nz, nt, nc = groups * share, groups // 2, hidden // TILE, depth // TILE
    f32, bf16 = jnp.float32, jnp.bfloat16
    any_space, vmem = pl.BlockSpec(memory_space=pl.ANY), pl.BlockSpec(memory_space=pltpu.VMEM)
    smem = pl.BlockSpec(memory_space=pltpu.SMEM)
    dma = pltpu.SemaphoreType.DMA
    half = rows // 2
    mixed = pl.pallas_call(
        functools.partial(fused_kernel, nz, nt),
        out_shape=jax.ShapeDtypeStruct(tokens.shape, f32),
        in_specs=[any_space, any_space, any_space, vmem, smem],
        out_specs=vmem,
        scratch_shapes=[
            pltpu.VMEM((steps, rows, depth), bf16),
            pltpu.VMEM((nt, depth, TILE), bf16),
            pltpu.VMEM((steps * nt, rows, TILE), f32),
            pltpu.VMEM((steps * nt, half, TILE), f32),
            pltpu.VMEM((steps * nt, half, TILE), bf16),
            pltpu.VMEM((steps * nt, half, TILE), bf16),
            pltpu.VMEM((steps, rows, hidden), bf16),
            pltpu.VMEM((steps, rows, depth), f32),
        ]
        + [pltpu.VMEM((steps * nc, nz, share, TILE), bf16)] * 2
        + [pltpu.VMEM((steps * nc * nz, share, TILE), bf16)] * 2
        + [
            dma((steps,)),
            dma((nt,)),
            dma((steps, 2 * nz - 1)),
            dma((steps, 2 * nz)),
        ]
        + [dma((steps * nt,))] * 6
        + [dma((steps * nc,))] * 2
        + [dma((steps * nc * nz,))] * 2,
        compiler_params=pltpu.CompilerParams(
            collective_id=0, has_side_effects=True, vmem_limit_bytes=67043328
        ),
    )(tokens, up_weight, down_weight, up_bias, active)
    return (mixed + down_bias.astype(f32)).astype(bf16)


def solution(mesh):
    placed = (
        P(None, "dp", "tensor"),
        P("tensor", "dp"),
        P("dp"),
        P("dp", "tensor"),
        P("tensor"),
        P(None, None, "dp"),
    )
    groups, columns = mesh.shape["dp"], mesh.shape["tensor"]

    def body(*args):
        steps, share, depth = args[0].shape
        hidden, table = args[1].shape[1], args[5].shape
        if (
            (groups, columns, steps, table[1]) == (8, 4, 2, 1)
            and share % 16 == 0
            and depth % TILE == 0
            and hidden % depth == 0
            and (hidden // TILE) and table[2] % (hidden // TILE) == 0
            and depth // TILE > LAG
        ):
            return fused(groups, *args)
        return local(*args)

    return jax.shard_map(
        body, mesh=mesh, in_specs=placed, out_specs=P(None, "dp", "tensor"), check_vma=False
    )
```

```python
import functools

import jax
import jax.numpy as jnp
from jax import lax
from jax.experimental import pallas as pl
from jax.experimental.pallas import tpu as pltpu
from jax.sharding import PartitionSpec as P

RBLK = 128
TILE = 512
LAG = 3
MESH = pl.DeviceIdType.MESH


def activate(summed, up_bias, mask_table, first_row):
    row_count = summed.shape[0]
    blocks = mask_table.shape[1]
    row_ids = first_row + jnp.arange(row_count, dtype=jnp.int32)
    onehot = (
        row_ids[:, None] // RBLK == jnp.arange(mask_table.shape[0], dtype=jnp.int32)[None, :]
    ).astype(jnp.float32)
    row_mask = jnp.dot(onehot, mask_table.astype(jnp.float32))
    preact = jnp.maximum(summed + up_bias.astype(jnp.float32), 0.0)
    gated_rows = preact.reshape(row_count, blocks, -1) * row_mask[:, :, None]
    return gated_rows.reshape(row_count, -1).astype(jnp.bfloat16)


def local(tokens, up_weight, up_bias, down_weight, down_bias, active):
    results = []
    for step_index in range(tokens.shape[0]):
        local_rows = tokens[step_index]
        mask_table = active[step_index]
        partial_up = jnp.dot(
            lax.all_gather(local_rows, "dp", axis=0, tiled=True),
            up_weight,
            preferred_element_type=jnp.float32,
        )
        row_share = lax.psum_scatter(partial_up, "tensor", scatter_dimension=0, tiled=True)
        first_row = lax.axis_index("tensor") * row_share.shape[0]
        hidden_share = activate(row_share, up_bias, mask_table, first_row)
        hidden = lax.all_gather(hidden_share, "tensor", axis=0, tiled=True)
        mixed_rows = lax.psum_scatter(
            jnp.dot(hidden, down_weight, preferred_element_type=jnp.float32),
            "dp",
            scatter_dimension=0,
            tiled=True,
        )
        results.append((mixed_rows + down_bias.astype(jnp.float32)).astype(jnp.bfloat16))
    return jnp.stack(results)


def fused_kernel(nz, nt, tok, wu, wd, bias_u, active, out,
                 x_all, w, pbuf, crecv, xsend, xrecv, hid, acc, ysend, yrecv, zsend, zrecv,
                 tsem, wsem, ag_send, ag_recv, c_send, c_recv, x_send, x_recv, h_send, h_recv,
                 y_send, y_recv, z_send, z_recv):
    f32, bf16 = jnp.float32, jnp.bfloat16
    steps, share, depth = tok.shape
    rows = x_all.shape[1]
    half = rows // 2
    dp, t = lax.axis_index("dp"), lax.axis_index("tensor")
    z, y = dp // 2, dp % 2
    x, c = t // 2, t % 2
    y_peer = (z * 2 + 1 - y, t)
    x_peer = (dp, (1 - x) * 2 + c)
    c_peer = (dp, x * 2 + 1 - c)
    z_of = lambda k: lax.rem(z + k, nz)
    own = pl.ds(pl.multiple_of(c * half, half), half)
    other = pl.ds(pl.multiple_of((1 - c) * half, half), half)
    cols = lambda j: pl.ds(pl.multiple_of(j * TILE, TILE), TILE)
    nc = depth // TILE
    spans = nt // nc
    block = lambda d: pl.ds(pl.multiple_of(d * share, share), share)

    def rcopy(src, dst, ss, rs, dev):
        return pltpu.make_async_remote_copy(
            src_ref=src, dst_ref=dst, send_sem=ss, recv_sem=rs, device_id=dev, device_id_type=MESH
        )

    def up_load(j):
        return pltpu.make_async_copy(wu.at[:, cols(j)], w.at[j], wsem.at[j])

    def down_load(i):
        n, part = i // spans, i % spans
        lines = pl.ds(pl.multiple_of(part * depth, depth), depth)
        return pltpu.make_async_copy(wd.at[lines, cols(n)], w.at[i], wsem.at[i])

    mine = [pltpu.make_async_copy(tok.at[s], x_all.at[s, block(dp)], tsem.at[s]) for s in range(steps)]
    for copy in mine:
        copy.start()

    @pl.loop(0, nt)
    def _(j):
        up_load(j).start()

    barrier = pltpu.get_barrier_semaphore()
    peers = [y_peer, x_peer, c_peer] + [(z_of(k) * 2 + y, t) for k in range(1, nz)]
    for peer in peers:
        pl.semaphore_signal(barrier, inc=1, device_id=peer, device_id_type=MESH)
    pl.semaphore_wait(barrier, len(peers))

    def ag_copy(s, k, d, peer):
        view = x_all.at[s, block(d)]
        return rcopy(view, view, ag_send.at[s, k], ag_recv.at[s, d], peer)

    def ag_sends(s):
        mine[s].wait()
        ag_copy(s, 0, dp, y_peer).start()
        for k in range(1, nz):
            ag_copy(s, k, dp, (z_of(k) * 2 + y, t)).start()

    def ag_forward(s, k):
        d = z_of(k) * 2 + y
        ag_copy(s, k, d, y_peer).wait_recv()
        ag_copy(s, nz - 1 + k, d, y_peer).start()

    def ag_finish(s):
        for k in range(nz):
            ag_copy(s, k, z_of(k) * 2 + 1 - y, y_peer).wait_recv()

    def c_copy(q):
        return rcopy(pbuf.at[q, other], crecv.at[q], c_send.at[q], c_recv.at[q], c_peer)

    def x_copy(q):
        return rcopy(xsend.at[q], xrecv.at[q], x_send.at[q], x_recv.at[q], x_peer)

    def h_copy(s, j, lines):
        view, q = hid.at[s, lines, cols(j)], s * nt + j
        return rcopy(view, view, h_send.at[q], h_recv.at[q], c_peer)

    def up(s, j):
        q = s * nt + j
        pbuf[q] = jnp.dot(x_all[s], w[j], preferred_element_type=f32)
        c_copy(q).start()

    def mid(q):
        c_copy(q).wait_recv()
        total = pbuf[q, own] + crecv[q]
        crecv[q] = total
        xsend[q] = total.astype(bf16)
        x_copy(q).start()

    def act(s, j):
        q = s * nt + j
        x_copy(q).wait_recv()
        bias = bias_u[cols(j)].astype(f32).reshape(1, TILE)
        pre = jnp.maximum(crecv[q] + xrecv[q].astype(f32) + bias, 0.0)
        blocks = active.shape[2] // nt
        width = TILE // blocks
        for b in range(blocks):
            gate = active[s, 0, j * blocks + b].astype(f32)
            lanes = pl.ds(pl.multiple_of(j * TILE + b * width, width), width)
            hid[s, own, lanes] = (pre[:, b * width : (b + 1) * width] * gate).astype(bf16)
        h_copy(s, j, own).start()

    def hidden_ready(s):
        @pl.loop(0, nt)
        def _(j):
            h_copy(s, j, other).wait_recv()

    def y_copy(i):
        return rcopy(ysend.at[i], yrecv.at[i], y_send.at[i], y_recv.at[i], y_peer)

    def z_copy(i, k):
        q = i * nz + k
        return rcopy(zsend.at[q], zrecv.at[q], z_send.at[q], z_recv.at[q], (z_of(k) * 2 + y, t))

    def down(s, n):
        total = jnp.zeros((rows, TILE), f32)
        for part in range(spans):
            total += jnp.dot(
                hid[s, :, part * depth : (part + 1) * depth], w[n * spans + part], preferred_element_type=f32
            )
        acc[s, :, cols(n)] = total
        i = s * nc + n
        for zz in range(nz):
            ysend[i, zz] = acc[s, block(zz * 2 + 1 - y), cols(n)].astype(bf16)
        y_copy(i).start()

    def rs_z(s, n):
        i = s * nc + n
        y_copy(i).wait_recv()
        for k in range(1, nz):
            pair = acc[s, block(z_of(k) * 2 + y), cols(n)] + yrecv[i, z_of(k)].astype(f32)
            zsend[i * nz + k] = pair.astype(bf16)
            z_copy(i, k).start()

    def rs_finish(s, n):
        i = s * nc + n
        total = acc[s, block(dp), cols(n)] + yrecv[i, z].astype(f32)
        for k in range(1, nz):
            z_copy(i, k).wait_recv()
            total += zrecv[i * nz + k].astype(f32)
        out[s, :, cols(n)] = total

    ag_sends(0)
    for k in range(1, nz):
        ag_forward(0, k)
    ag_sends(1)
    ag_finish(0)

    def first_step(j):
        up_load(j).wait()
        up(0, j)

        @pl.when(j >= 1)
        def _():
            mid(j - 1)

    cut = [nt * k // (nz + 1) for k in range(nz)] + [nt]
    for k in range(nz):
        pl.loop(cut[k], cut[k + 1])(first_step)
        if k + 1 < nz:
            ag_forward(1, k + 1)
    mid(nt - 1)
    ag_finish(1)

    @pl.loop(0, nt)
    def _(j):
        up(1, j)

        @pl.when(j >= 1)
        def _():
            mid(nt + j - 1)
            down_load(j - 1).start()

        act(0, j)

    mid(2 * nt - 1)
    down_load(nt - 1).start()
    hidden_ready(0)

    @pl.loop(0, nc)
    def _(n):
        for part in range(spans):
            down_load(n * spans + part).wait()
        down(0, n)

        @pl.when(n >= LAG)
        def _():
            rs_z(0, n - LAG)

    @pl.loop(0, nt // 2)
    def _(j):
        act(1, j)

    @pl.loop(nc - LAG, nc)
    def _(n):
        rs_z(0, n)

    @pl.loop(nt // 2, nt)
    def _(j):
        act(1, j)

    @pl.loop(0, nc - LAG)
    def _(n):
        rs_finish(0, n)

    hidden_ready(1)

    @pl.loop(0, nc)
    def _(n):
        down(1, n)

        @pl.when(n < LAG)
        def _():
            rs_finish(0, nc - LAG + n)

        @pl.when(n >= LAG)
        def _():
            rs_z(1, n - LAG)

    @pl.loop(nc - LAG, nc)
    def _(n):
        rs_z(1, n)

    @pl.loop(0, nc)
    def _(n):
        rs_finish(1, n)

    for s in range(steps):
        for k in range(2 * nz - 1):
            ag_copy(s, k, dp, y_peer).wait_send()

    @pl.loop(0, steps * nc)
    def _(i):
        y_copy(i).wait_send()
        for k in range(1, nz):
            z_copy(i, k).wait_send()

    for s in range(steps):
        @pl.loop(0, nt)
        def _(j):
            c_copy(s * nt + j).wait_send()
            x_copy(s * nt + j).wait_send()
            h_copy(s, j, own).wait_send()


def fused(groups, tokens, up_weight, up_bias, down_weight, down_bias, active):
    steps, share, depth = tokens.shape
    hidden = up_weight.shape[1]
    rows, nz, nt, nc = groups * share, groups // 2, hidden // TILE, depth // TILE
    f32, bf16 = jnp.float32, jnp.bfloat16
    any_space, vmem = pl.BlockSpec(memory_space=pl.ANY), pl.BlockSpec(memory_space=pltpu.VMEM)
    smem = pl.BlockSpec(memory_space=pltpu.SMEM)
    dma = pltpu.SemaphoreType.DMA
    half = rows // 2
    mixed = pl.pallas_call(
        functools.partial(fused_kernel, nz, nt),
        out_shape=jax.ShapeDtypeStruct(tokens.shape, f32),
        in_specs=[any_space, any_space, any_space, vmem, smem],
        out_specs=vmem,
        scratch_shapes=[
            pltpu.VMEM((steps, rows, depth), bf16),
            pltpu.VMEM((nt, depth, TILE), bf16),
            pltpu.VMEM((steps * nt, rows, TILE), f32),
            pltpu.VMEM((steps * nt, half, TILE), f32),
            pltpu.VMEM((steps * nt, half, TILE), bf16),
            pltpu.VMEM((steps * nt, half, TILE), bf16),
            pltpu.VMEM((steps, rows, hidden), bf16),
            pltpu.VMEM((steps, rows, depth), f32),
        ]
        + [pltpu.VMEM((steps * nc, nz, share, TILE), bf16)] * 2
        + [pltpu.VMEM((steps * nc * nz, share, TILE), bf16)] * 2
        + [
            dma((steps,)),
            dma((nt,)),
            dma((steps, 2 * nz - 1)),
            dma((steps, 2 * nz)),
        ]
        + [dma((steps * nt,))] * 6
        + [dma((steps * nc,))] * 2
        + [dma((steps * nc * nz,))] * 2,
        compiler_params=pltpu.CompilerParams(
            collective_id=0, has_side_effects=True, vmem_limit_bytes=67043328
        ),
    )(tokens, up_weight, down_weight, up_bias, active)
    return (mixed + down_bias.astype(f32)).astype(bf16)


def solution(mesh):
    placed = (
        P(None, "dp", "tensor"),
        P("tensor", "dp"),
        P("dp"),
        P("dp", "tensor"),
        P("tensor"),
        P(None, None, "dp"),
    )
    groups, columns = mesh.shape["dp"], mesh.shape["tensor"]

    def body(*args):
        steps, share, depth = args[0].shape
        hidden, table = args[1].shape[1], args[5].shape
        if (
            (groups, columns, steps, table[1]) == (8, 4, 2, 1)
            and share % 16 == 0
            and depth % TILE == 0
            and hidden % depth == 0
            and (hidden // TILE) and table[2] % (hidden // TILE) == 0
            and depth // TILE > LAG
        ):
            return fused(groups, *args)
        return local(*args)

    return jax.shard_map(
        body, mesh=mesh, in_specs=placed, out_specs=P(None, "dp", "tensor"), check_vma=False
    )
```
